128 devices in a mesh: gz: 4 (over z), gx: 4 (over y_lo, core), gy: 8 (over x, y_hi).
Axes of the slice: x: 4, y: 4 (y_hi: 2, y_lo: 2; y = y_hi * 2 + y_lo), z: 4, core: 2. Of those that a mesh axis runs over, the one named last changes fastest.
Arguments:
- right_side: float32 [40, 128, 6, 1024], P('gz', 'gy', None, 'gx'), may hold values from -0.0625 to 0.0625
- previous: float32 [40, 128, 6, 1024], P('gz', 'gy', None, 'gx'), may hold values from -0.15625 to 0.15625
- diag_inverse: bfloat16 [40, 128, 6, 6, 1024], P('gz', 'gy', None, None, 'gx'), may hold values from -0.6 to 2.6, as said below
- jacobians: bfloat16 [40, 128, 6, 6, 6, 1024], P('gz', 'gy', None, None, None, 'gx'), may hold values from -3 to 3, as said below
Outputs:
- update: float32 [40, 128, 6, 1024], P('gz', 'gy', None, 'gx')
The draws below stay inside these ranges and needn't reach their ends.
Inputs may be any that keep to these rules, and one draw needn't show every extreme that they name: `diag_inverse`: entries of the cells' inverted diagonal blocks. `jacobians`: entries of the cells' coupling blocks.
All inputs are finite; a program needn't handle non-finite values.
Results may differ from the reference program's by a relative error of at most 0.0003.
Values sent between devices are 32-bit elements; how exact they have to be, the bound alone decides.
A program may use at most 128 MiB of HBM per device.

```python
import math
import jax
import jax.numpy as jnp
from jax import lax

VARS = 6
NX = 1024
NY = 128
DEPTH_LAYERS = 40


def cell_blocks(key):
    base = jax.random.fold_in(key, 4711)
    parallel_columns = jax.random.split(base, 10)
    unit = jnp.eye(6, dtype=jnp.float32)[:, :, None]
    scale = jnp.exp(jax.random.uniform(parallel_columns[0], (DEPTH_LAYERS, NY, 1, 1, NX), minval=math.log(0.5), maxval=math.log(2.0)))
    offdiag = 0.07 * jnp.clip(jax.random.normal(parallel_columns[1], (DEPTH_LAYERS, NY, 6, 6, NX)), -4.0, 4.0) * (1.0 - unit)
    inverse = scale * (unit + offdiag)
    series = jnp.broadcast_to(unit, (DEPTH_LAYERS, NY, 6, 6, NX))
    for term_index in range(4):
        series = unit - jnp.einsum('zyabx,zybcx->zyacx', offdiag, series)
    fraction = 0.5
    slow = jax.random.uniform(parallel_columns[2], (1, NY, 1, 1, NX)) < fraction
    cell_shape = (DEPTH_LAYERS, NY, 1, 1, NX)
    rate_lower = jnp.where(slow, jax.random.uniform(parallel_columns[3], cell_shape, minval=0.99, maxval=0.998), jax.random.uniform(parallel_columns[4], cell_shape, minval=0.92, maxval=0.96))
    rate_upper = jnp.where(slow, jax.random.uniform(parallel_columns[5], cell_shape, minval=0.99, maxval=0.998), jax.random.uniform(parallel_columns[6], cell_shape, minval=0.92, maxval=0.96))
    layer_indices = jnp.arange(DEPTH_LAYERS)
    forward_triangular_solve = jax.random.randint(parallel_columns[7], (2,), 0, DEPTH_LAYERS)
    backward_triangular_solve = jax.random.randint(parallel_columns[8], (2,), 0, DEPTH_LAYERS)
    subdiagonal_matrices = jnp.where(jnp.any(layer_indices[:, None] == forward_triangular_solve[None, :], axis=1), 0.7, 1.0).reshape(DEPTH_LAYERS, 1, 1, 1, 1)
    superdiagonal_matrices = jnp.where(jnp.any(layer_indices[:, None] == backward_triangular_solve[None, :], axis=1), 0.7, 1.0).reshape(DEPTH_LAYERS, 1, 1, 1, 1)
    lower_z = -(rate_lower * subdiagonal_matrices / scale) * series
    upper_z = -(rate_upper * superdiagonal_matrices / scale) * series
    neighbours = 0.1 * jnp.clip(jax.random.normal(parallel_columns[9], (DEPTH_LAYERS, NY, 4, 6, 6, NX)), -5.0, 5.0)
    coupling = jnp.concatenate([neighbours, lower_z[:, :, None], upper_z[:, :, None]], axis=2)
    return (inverse, coupling)


def draw_diag_inverse(key, part):
    inverse, coupling = cell_blocks(key)
    return inverse.astype(jnp.bfloat16)


def draw_jacobians(key, part):
    inverse, coupling = cell_blocks(key)
    return coupling.astype(jnp.bfloat16)


def block_scale(rng, shape, cuts, low, top_value):
    def one(position, blocks):
        heights = jax.random.uniform(jax.random.fold_in(jax.random.fold_in(rng, 6), position), (blocks,), jnp.float32, low / len(cuts), top_value / len(cuts))
        return jnp.repeat(jnp.exp(heights), shape[position] // blocks).reshape((-1,) + (1,) * (len(shape) - position - 1))

    loudness = one(*cuts[0])
    for cut in cuts[1:]:
        loudness = loudness * one(*cut)
    return loudness


def centred(stream_key, extent, scale, limit, shards=(), kind=jnp.bfloat16):
    values = jax.random.normal(stream_key, extent, jnp.float32) * scale
    if len(shards) > 0:
        values = block_scale(stream_key, extent, shards, -0.22, 0.18) * values
    return jnp.clip(values, min=-limit, max=limit).astype(kind)


def setup_inputs(seed: int = 0) -> dict:
    key_list = jax.random.split(jax.random.key(seed), 5)
    right_side = centred(key_list[0], (DEPTH_LAYERS, NY, VARS, NX), 0.004, 0.0625, ((0, 4), (1, 8), (3, 4)), jnp.float32)
    previous = centred(key_list[1], (DEPTH_LAYERS, NY, VARS, NX), 0.01, 0.15625, ((0, 4), (1, 8), (3, 4)), jnp.float32)
    diag_inverse = draw_diag_inverse(jax.random.fold_in(key_list[4], 71), 0)
    jacobians = draw_jacobians(jax.random.fold_in(key_list[4], 71), 0)
    return dict(right_side=right_side, previous=previous, diag_inverse=diag_inverse, jacobians=jacobians)


def block_apply(blocks, vector):
    return jnp.sum(blocks * vector[..., None, :, :], axis=-2)


def inplane_terms(coupling, padded):
    total = block_apply(coupling[:, 0], padded[1:-1, :, :-2])
    total = total + block_apply(coupling[:, 1], padded[1:-1, :, 2:])
    total = total + block_apply(coupling[:, 2], padded[:-2, :, 1:-1])
    total = total + block_apply(coupling[:, 3], padded[2:, :, 1:-1])
    return total


def pad_plane(plane):
    return jnp.pad(plane, ((1, 1), (0, 0), (1, 1)))


def reference(right_side, previous, diag_inverse, jacobians):
    zeros_plane = jnp.zeros((NY, 6, NX), jnp.float32)

    def forward_step(earlier, planes):
        source, before, inverse, coupling = planes
        inverse = inverse.astype(jnp.float32)
        coupling = coupling.astype(jnp.float32)
        source = source - inplane_terms(coupling, pad_plane(before)) - block_apply(coupling[:, 4], earlier)
        result = block_apply(inverse, source)
        return result, result

    final_plane, sweep_values = lax.scan(forward_step, zeros_plane, (right_side, previous, diag_inverse, jacobians))

    def backward_step(later, planes):
        forward_plane, before, inverse, coupling = planes
        inverse = inverse.astype(jnp.float32)
        coupling = coupling.astype(jnp.float32)
        change = block_apply(coupling[:, 5], later) + inplane_terms(coupling, pad_plane(forward_plane - before))
        result = forward_plane - block_apply(inverse, change)
        return result, result

    last_plane, update = lax.scan(backward_step, zeros_plane, (sweep_values, previous, diag_inverse, jacobians), reverse=True)
    return update
```

```python
import functools

import jax
import jax.numpy as jnp
from jax import lax
from jax.experimental import pallas as pl
from jax.experimental.pallas import tpu as pltpu
from jax.sharding import PartitionSpec as P

F32 = jnp.float32
V = 6
TILE_Y, TILE_X = 8, 128
CHUNKS = ((0, 0), (1, 0), (0, 1), (1, 1))


def kernel(sizes, rhs_h, prev_h, dinv_h, jac_h, out_ref, jv, dv, rv, pv, sv,
           send_y, recv_y, send_x, recv_x, send_z, recv_z,
           ld_p, ld_r, ld_j, ld_l, ld_d, ld_u, ssy, rsy, ssx, rsx, ssz, rsz):
    nz, nx, ny = sizes
    planes, _, rows, cols = rhs_h.shape
    iz, ix, iy = (lax.axis_index(a) for a in ("gz", "gx", "gy"))

    load_prev = pltpu.make_async_copy(prev_h, pv, ld_p)
    load_prev.start()

    def load_first(z):
        return (
            pltpu.make_async_copy(jac_h.at[z, pl.ds(0, 4)], jv.at[z, pl.ds(0, 4)], ld_j.at[z]),
            pltpu.make_async_copy(rhs_h.at[z], rv.at[z], ld_r.at[z]),
        )

    def load_lower(z):
        return (
            pltpu.make_async_copy(jac_h.at[z, 4], jv.at[z, 4], ld_l.at[z]),
            pltpu.make_async_copy(dinv_h.at[z], dv.at[z], ld_d.at[z]),
        )

    def load_upper(z):
        return (pltpu.make_async_copy(jac_h.at[z, 5], jv.at[z, 5], ld_u.at[z]),)

    for group in (load_first, load_lower, load_upper):

        @pl.loop(0, planes)
        def _(z):
            for copy in group(z):
                copy.start()

    sides = (
        ("gy", -1, iy > 0), ("gy", 1, iy < ny - 1),
        ("gx", -1, ix > 0), ("gx", 1, ix < nx - 1),
        ("gz", -1, iz > 0), ("gz", 1, iz < nz - 1),
    )
    at = {"gz": iz, "gx": ix, "gy": iy}
    barrier = pltpu.get_barrier_semaphore()
    for axis, step, exists in sides:

        @pl.when(exists)
        def _():
            pl.semaphore_signal(
                barrier, inc=1, device_id={axis: at[axis] + step},
                device_id_type=pl.DeviceIdType.MESH)

    def copy_y(e, yh, xh):
        step = 2 * yh - 1
        return pltpu.make_async_remote_copy(
            send_y.at[e, yh, xh], recv_y.at[e, 1 - yh, xh], ssy.at[e, yh, xh],
            rsy.at[e, 1 - yh, xh], device_id={"gy": iy + step},
            device_id_type=pl.DeviceIdType.MESH)

    def copy_x(e, yh, xh):
        step = 2 * xh - 1
        return pltpu.make_async_remote_copy(
            send_x.at[e, xh, yh], recv_x.at[e, 1 - xh, yh], ssx.at[e, xh, yh],
            rsx.at[e, 1 - xh, yh], device_id={"gx": ix + step},
            device_id_type=pl.DeviceIdType.MESH)

    def copy_z(d, c):
        step = 1 - 2 * d
        return pltpu.make_async_remote_copy(
            send_z.at[d, c], recv_z.at[d, c], ssz.at[d, c], rsz.at[d, c],
            device_id={"gz": iz + step}, device_id_type=pl.DeviceIdType.MESH)

    has_y = (iy > 0, iy < ny - 1)
    has_x = (ix > 0, ix < nx - 1)

    def start_faces(e, yh, xh):
        @pl.when(has_y[yh])
        def _():
            copy_y(e, yh, xh).start()

        @pl.when(has_x[xh])
        def _():
            copy_x(e, yh, xh).start()

    def wait_faces(e, yh, xh):
        @pl.when(has_y[yh])
        def _():
            copy_y(e, 1 - yh, xh).wait_recv()

        @pl.when(has_x[xh])
        def _():
            copy_x(e, yh, 1 - xh).wait_recv()

    for side in range(2):

        @pl.when(jnp.logical_not(has_y[side]))
        def _():
            for e in range(2):
                for xh in range(2):
                    recv_y[e, side, xh] = jnp.zeros(recv_y.shape[3:], F32)

        @pl.when(jnp.logical_not(has_x[side]))
        def _():
            for e in range(2):
                for yh in range(2):
                    recv_x[e, side, yh] = jnp.zeros(recv_x.shape[3:], F32)

    lane8 = lax.broadcasted_iota(jnp.int32, (TILE_Y, TILE_X), 1)
    row8 = lax.broadcasted_iota(jnp.int32, (TILE_Y, TILE_X), 0)

    def cut(yh, xh):
        return pl.ds(yh * TILE_Y, TILE_Y), pl.ds(xh * TILE_X, TILE_X)

    def pack_faces(e, yh, xh, z, values, packed):
        for v in range(V):
            index = z * V + v
            edge = (TILE_Y - 1) * yh
            send_y[e, yh, xh, index] = values[v][edge:edge + 1, :]
            packed = jnp.where(
                lane8 == index, pltpu.roll(values[v], lax.rem(index + xh, TILE_X), 1), packed)
        return packed

    load_prev.wait()
    for yh, xh in CHUNKS:
        ys, xs = cut(yh, xh)

        def pack(z, packed):
            return pack_faces(0, yh, xh, z, [pv[z, v, ys, xs] for v in range(V)], packed)

        send_x[0, xh, yh] = lax.fori_loop(0, planes, pack, jnp.zeros((TILE_Y, TILE_X), F32))

    pl.semaphore_wait(barrier, sum(exists.astype(jnp.int32) for _, _, exists in sides))

    for yh, xh in CHUNKS:
        start_faces(0, yh, xh)

    lane = lax.broadcasted_iota(jnp.int32, (rows, cols), 1)
    row = lax.broadcasted_iota(jnp.int32, (rows, cols), 0)
    shifts = (
        (lane == 0, 1, 1), (lane == cols - 1, cols - 1, 1),
        (row == 0, 1, 0), (row == rows - 1, rows - 1, 0),
    )

    def interior(z, subtract):
        f = [pv[z, v] for v in range(V)]
        for n, (edge, shift, axis) in enumerate(shifts):
            g = [jnp.where(edge, 0.0, pltpu.roll(x, shift, axis)) for x in f]
            for a in range(V):
                total = jv[z, n, a, 0].astype(F32) * g[0]
                for b in range(1, V):
                    total = total + jv[z, n, a, b].astype(F32) * g[b]
                if subtract:
                    rv[z, a] = rv[z, a] - total
                elif n == 0:
                    rv[z, a] = total
                else:
                    rv[z, a] = rv[z, a] + total

    def matvec(blocks, vector):
        out = []
        for a in range(V):
            terms = [blocks(a, b).astype(F32) * vector[b] for b in range(V)]
            out.append(((terms[0] + terms[1]) + (terms[2] + terms[3])) + (terms[4] + terms[5]))
        return out

    def add_halo(e, yh, xh, sign):
        ys, xs = cut(yh, xh)
        wait_faces(e, yh, xh)
        packed = recv_x[e, xh, yh]
        on_row = row8 == (TILE_Y - 1) * yh
        on_lane = lane8 == (TILE_X - 1) * xh

        @pl.loop(0, planes)
        def _(z):
            hy, hx = [], []
            for v in range(V):
                index = z * V + v
                hy.append(jnp.where(on_row, recv_y[e, yh, xh, index], 0.0))
                turn = lax.rem(TILE_X + (TILE_X - 1) * xh - index, TILE_X)
                hx.append(jnp.where(on_lane, pltpu.roll(packed, turn, 1), 0.0))
            fx = matvec(lambda a, b: jv[z, xh, a, b, ys, xs], hx)
            fy = matvec(lambda a, b: jv[z, 2 + yh, a, b, ys, xs], hy)
            for a in range(V):
                rv[z, a, ys, xs] = rv[z, a, ys, xs] + sign * (fx[a] + fy[a])

    def sweep_up(c, incoming):
        yh, xh = CHUNKS[c]
        ys, xs = cut(yh, xh)

        def step(z, carry):
            below, packed = carry
            lower = matvec(lambda a, b: jv[z, 4, a, b, ys, xs], below)
            source = [rv[z, a, ys, xs] - lower[a] for a in range(V)]
            result = matvec(lambda a, b: dv[z, a, b, ys, xs], source)
            change = []
            for a in range(V):
                sv[z, a, ys, xs] = result[a]
                change.append(result[a] - pv[z, a, ys, xs])
                pv[z, a, ys, xs] = change[a]
            return tuple(result), pack_faces(1, yh, xh, z, change, packed)

        top, packed = lax.fori_loop(
            0, planes, step, (tuple(incoming), jnp.zeros((TILE_Y, TILE_X), F32)))
        for v in range(V):
            send_z[0, c, v] = top[v]
        send_x[1, xh, yh] = packed

        @pl.when(iz < nz - 1)
        def _():
            copy_z(0, c).start()

        start_faces(1, yh, xh)

    def sweep_down(c, incoming):
        ys, xs = cut(*CHUNKS[c])

        def step(i, above):
            z = planes - 1 - i
            upper = matvec(lambda a, b: jv[z, 5, a, b, ys, xs], above)
            change = [rv[z, a, ys, xs] + upper[a] for a in range(V)]
            change = matvec(lambda a, b: dv[z, a, b, ys, xs], change)
            result = [sv[z, a, ys, xs] - change[a] for a in range(V)]
            for a in range(V):
                out_ref[z, a, ys, xs] = result[a]
            return tuple(result)

        bottom = lax.fori_loop(0, planes, step, tuple(incoming))
        for v in range(V):
            send_z[1, c, v] = bottom[v]

        @pl.when(iz > 0)
        def _():
            copy_z(1, c).start()

    zeros = [jnp.zeros((TILE_Y, TILE_X), F32)] * V

    @pl.loop(0, planes)
    def _(z):
        for copy in load_first(z):
            copy.wait()
        interior(z, True)

    @pl.loop(0, planes)
    def _(z):
        for copy in load_lower(z):
            copy.wait()

    for c, (yh, xh) in enumerate(CHUNKS):
        add_halo(0, yh, xh, -1.0)

        @pl.when(iz == 0)
        def _():
            sweep_up(c, zeros)

    @pl.when(iz > 0)
    def _():
        for c in range(len(CHUNKS)):
            copy_z(0, c).wait_recv()
            sweep_up(c, [recv_z[0, c, v] for v in range(V)])

    @pl.loop(0, planes)
    def _(z):
        interior(z, False)

    @pl.loop(0, planes)
    def _(z):
        for copy in load_upper(z):
            copy.wait()

    for c, (yh, xh) in enumerate(CHUNKS):
        add_halo(1, yh, xh, 1.0)

        @pl.when(iz == nz - 1)
        def _():
            sweep_down(c, zeros)

    @pl.when(iz < nz - 1)
    def _():
        for c in range(len(CHUNKS)):
            copy_z(1, c).wait_recv()
            sweep_down(c, [recv_z[1, c, v] for v in range(V)])

    for e in range(2):
        for yh, xh in CHUNKS:

            @pl.when(has_y[yh])
            def _():
                copy_y(e, yh, xh).wait_send()

            @pl.when(has_x[xh])
            def _():
                copy_x(e, yh, xh).wait_send()

    for c in range(len(CHUNKS)):

        @pl.when(iz < nz - 1)
        def _():
            copy_z(0, c).wait_send()

        @pl.when(iz > 0)
        def _():
            copy_z(1, c).wait_send()


def body(sizes, right_side, previous, diag_inverse, jacobians):
    rhs = jnp.transpose(right_side, (0, 2, 1, 3))
    prev = jnp.transpose(previous, (0, 2, 1, 3))
    dinv = jnp.transpose(diag_inverse, (0, 2, 3, 1, 4))
    jac = jnp.transpose(jacobians, (0, 2, 3, 4, 1, 5))
    planes, _, rows, cols = rhs.shape
    faces = planes * V
    n = len(CHUNKS)
    hbm = pl.BlockSpec(memory_space=pl.ANY)
    dma = pltpu.SemaphoreType.DMA
    out = pl.pallas_call(
        functools.partial(kernel, sizes),
        out_shape=jax.ShapeDtypeStruct(rhs.shape, F32),
        in_specs=[hbm] * 4,
        out_specs=pl.BlockSpec(memory_space=pltpu.VMEM),
        scratch_shapes=[
            pltpu.VMEM(jac.shape, jac.dtype),
            pltpu.VMEM(dinv.shape, dinv.dtype),
            pltpu.VMEM(rhs.shape, F32),
            pltpu.VMEM(rhs.shape, F32),
            pltpu.VMEM(rhs.shape, F32),
            pltpu.VMEM((2, 2, 2, faces, 1, TILE_X), F32),
            pltpu.VMEM((2, 2, 2, faces, 1, TILE_X), F32),
            pltpu.VMEM((2, 2, 2, TILE_Y, TILE_X), F32),
            pltpu.VMEM((2, 2, 2, TILE_Y, TILE_X), F32),
            pltpu.VMEM((2, n, V, TILE_Y, TILE_X), F32),
            pltpu.VMEM((2, n, V, TILE_Y, TILE_X), F32),
            dma, dma((planes,)), dma((planes,)), dma((planes,)), dma((planes,)), dma((planes,)),
            dma((2, 2, 2)), dma((2, 2, 2)), dma((2, 2, 2)), dma((2, 2, 2)),
            dma((2, n)), dma((2, n)),
        ],
        compiler_params=pltpu.CompilerParams(
            collective_id=0, has_side_effects=True, vmem_limit_bytes=60 * 1024 * 1024),
        name="sweep_pair",
    )(rhs, prev, dinv, jac)
    return jnp.transpose(out, (0, 2, 1, 3))


def solution(mesh):
    placed = (
        P("gz", "gy", None, "gx"),
        P("gz", "gy", None, "gx"),
        P("gz", "gy", None, None, "gx"),
        P("gz", "gy", None, None, None, "gx"),
    )
    sizes = tuple(mesh.shape[a] for a in ("gz", "gx", "gy"))
    return jax.shard_map(
        functools.partial(body, sizes), mesh=mesh, in_specs=placed,
        out_specs=P("gz", "gy", None, "gx"), check_vma=False,
    )
```

```python
import functools

import jax
import jax.numpy as jnp
from jax import lax
from jax.experimental import pallas as pl
from jax.experimental.pallas import tpu as pltpu
from jax.sharding import PartitionSpec as P

F32 = jnp.float32
V = 6
TILE_Y, TILE_X = 8, 128
PLANES_AT_ONCE = 5
CHUNKS = ((0, 0), (1, 0), (0, 1), (1, 1))


def kernel(sizes, rhs_h, prev_h, dinv_h, jac_h, out_ref, jv, dv, rv, pv, sv,
           send_y, recv_y, send_x, recv_x, send_z, recv_z,
           ld_p, ld_r, ld_j, ld_l, ld_d, ld_u, ssy, rsy, ssx, rsx, ssz, rsz):
    nz, nx, ny = sizes
    planes, _, rows, cols = rhs_h.shape
    iz, ix, iy = (lax.axis_index(a) for a in ("gz", "gx", "gy"))

    load_prev = pltpu.make_async_copy(prev_h, pv, ld_p)
    load_prev.start()

    def load_first(z):
        return (
            pltpu.make_async_copy(jac_h.at[z, pl.ds(0, 4)], jv.at[z, pl.ds(0, 4)], ld_j.at[z]),
            pltpu.make_async_copy(rhs_h.at[z], rv.at[z], ld_r.at[z]),
        )

    def load_lower(z):
        return (
            pltpu.make_async_copy(jac_h.at[z, 4], jv.at[z, 4], ld_l.at[z]),
            pltpu.make_async_copy(dinv_h.at[z], dv.at[z], ld_d.at[z]),
        )

    def load_upper(z):
        return (pltpu.make_async_copy(jac_h.at[z, 5], jv.at[z, 5], ld_u.at[z]),)

    for group in (load_first, load_lower, load_upper):

        @pl.loop(0, planes)
        def _(z):
            for copy in group(z):
                copy.start()

    sides = (
        ("gy", -1, iy > 0), ("gy", 1, iy < ny - 1),
        ("gx", -1, ix > 0), ("gx", 1, ix < nx - 1),
        ("gz", -1, iz > 0), ("gz", 1, iz < nz - 1),
    )
    at = {"gz": iz, "gx": ix, "gy": iy}
    barrier = pltpu.get_barrier_semaphore()
    for axis, step, exists in sides:

        @pl.when(exists)
        def _():
            pl.semaphore_signal(
                barrier, inc=1, device_id={axis: at[axis] + step},
                device_id_type=pl.DeviceIdType.MESH)

    def copy_y(e, yh, xh):
        step = 2 * yh - 1
        return pltpu.make_async_remote_copy(
            send_y.at[e, yh, xh], recv_y.at[e, 1 - yh, xh], ssy.at[e, yh, xh],
            rsy.at[e, 1 - yh, xh], device_id={"gy": iy + step},
            device_id_type=pl.DeviceIdType.MESH)

    def copy_x(e, yh, xh):
        step = 2 * xh - 1
        return pltpu.make_async_remote_copy(
            send_x.at[e, xh, yh], recv_x.at[e, 1 - xh, yh], ssx.at[e, xh, yh],
            rsx.at[e, 1 - xh, yh], device_id={"gx": ix + step},
            device_id_type=pl.DeviceIdType.MESH)

    def copy_z(d, c):
        step = 1 - 2 * d
        return pltpu.make_async_remote_copy(
            send_z.at[d, c], recv_z.at[d, c], ssz.at[d, c], rsz.at[d, c],
            device_id={"gz": iz + step}, device_id_type=pl.DeviceIdType.MESH)

    has_y = (iy > 0, iy < ny - 1)
    has_x = (ix > 0, ix < nx - 1)

    def start_faces(e, yh, xh):
        @pl.when(has_y[yh])
        def _():
            copy_y(e, yh, xh).start()

        @pl.when(has_x[xh])
        def _():
            copy_x(e, yh, xh).start()

    def wait_faces(e, yh, xh):
        @pl.when(has_y[yh])
        def _():
            copy_y(e, 1 - yh, xh).wait_recv()

        @pl.when(has_x[xh])
        def _():
            copy_x(e, yh, 1 - xh).wait_recv()

    lane8 = lax.broadcasted_iota(jnp.int32, (TILE_Y, TILE_X), 1)
    row8 = lax.broadcasted_iota(jnp.int32, (TILE_Y, TILE_X), 0)

    def cut(yh, xh):
        return pl.ds(yh * TILE_Y, TILE_Y), pl.ds(xh * TILE_X, TILE_X)

    def pack_faces(e, yh, xh):
        ys, xs = cut(yh, xh)
        edge = yh * (rows - 1)
        packed = [jnp.zeros((TILE_Y, TILE_X), F32) for _ in range(4)]
        for index in range(planes * V):
            z, v = divmod(index, V)
            send_y[e, yh, xh, index] = pv[z, v, edge:edge + 1, xs]
            turned = pltpu.roll(pv[z, v, ys, xs], index + 2 * xh, 1)
            packed[index % 4] = jnp.where(lane8 == index + xh, turned, packed[index % 4])
        send_x[e, xh, yh] = (packed[0] + packed[1]) + (packed[2] + packed[3])

    def unrolled(step, carry, upward=True):
        def turn(i, carry):
            for j in range(PLANES_AT_ONCE):
                at = i * PLANES_AT_ONCE + j
                carry = step(at if upward else planes - 1 - at, carry)
            return carry

        return lax.fori_loop(0, planes // PLANES_AT_ONCE, turn, carry)

    load_prev.wait()
    for yh, xh in CHUNKS:
        pack_faces(0, yh, xh)

    pl.semaphore_wait(barrier, sum(exists.astype(jnp.int32) for _, _, exists in sides))

    for yh, xh in CHUNKS:
        start_faces(0, yh, xh)

    for side in range(2):

        @pl.when(jnp.logical_not(has_y[side]))
        def _():
            for e in range(2):
                for xh in range(2):
                    recv_y[e, side, xh] = jnp.zeros(recv_y.shape[3:], F32)

        @pl.when(jnp.logical_not(has_x[side]))
        def _():
            for e in range(2):
                for yh in range(2):
                    recv_x[e, side, yh] = jnp.zeros(recv_x.shape[3:], F32)

    @pl.when(iz == 0)
    def _():
        recv_z[0] = jnp.zeros(recv_z.shape[1:], F32)

    @pl.when(iz == nz - 1)
    def _():
        recv_z[1] = jnp.zeros(recv_z.shape[1:], F32)

    lane = lax.broadcasted_iota(jnp.int32, (rows, cols), 1)
    row = lax.broadcasted_iota(jnp.int32, (rows, cols), 0)
    shifts = (
        (lane == 0, 1, 1), (lane == cols - 1, cols - 1, 1),
        (row == 0, 1, 0), (row == rows - 1, rows - 1, 0),
    )

    def interior(z, subtract):
        f = [pv[z, v] for v in range(V)]
        for n, (edge, shift, axis) in enumerate(shifts):
            g = [jnp.where(edge, 0.0, pltpu.roll(x, shift, axis)) for x in f]
            for a in range(V):
                total = jv[z, n, a, 0].astype(F32) * g[0]
                for b in range(1, V):
                    total = total + jv[z, n, a, b].astype(F32) * g[b]
                if subtract:
                    rv[z, a] = rv[z, a] - total
                elif n == 0:
                    rv[z, a] = total
                else:
                    rv[z, a] = rv[z, a] + total

    def matvec(blocks, vector):
        out = []
        for a in range(V):
            terms = [blocks(a, b).astype(F32) * vector[b] for b in range(V)]
            out.append(((terms[0] + terms[1]) + (terms[2] + terms[3])) + (terms[4] + terms[5]))
        return out

    def add_halo(e, yh, xh):
        ys, xs = cut(yh, xh)
        wait_faces(e, yh, xh)
        packed = recv_x[e, xh, yh]
        on_row = row8 == (TILE_Y - 1) * yh
        on_lane = lane8 == (TILE_X - 1) * xh

        def step(z, carry):
            hy, hx = [], []
            for v in range(V):
                index = z * V + v
                hy.append(jnp.where(on_row, recv_y[e, yh, xh, index], 0.0))
                hx.append(jnp.where(on_lane, pltpu.roll(packed, TILE_X - 1 - index, 1), 0.0))
            fx = matvec(lambda a, b: jv[z, xh, a, b, ys, xs], hx)
            fy = matvec(lambda a, b: jv[z, 2 + yh, a, b, ys, xs], hy)
            for a in range(V):
                if e == 0:
                    rv[z, a, ys, xs] = rv[z, a, ys, xs] - (fx[a] + fy[a])
                else:
                    rv[z, a, ys, xs] = rv[z, a, ys, xs] + (fx[a] + fy[a])
            return carry

        unrolled(step, 0)

    def sweep_up(c):
        yh, xh = CHUNKS[c]
        ys, xs = cut(yh, xh)

        @pl.when(iz > 0)
        def _():
            copy_z(0, c).wait_recv()

        def step(z, below):
            lower = matvec(lambda a, b: jv[z, 4, a, b, ys, xs], below)
            source = [rv[z, a, ys, xs] - lower[a] for a in range(V)]
            result = matvec(lambda a, b: dv[z, a, b, ys, xs], source)
            for a in range(V):
                sv[z, a, ys, xs] = result[a]
                pv[z, a, ys, xs] = result[a] - pv[z, a, ys, xs]
            return tuple(result)

        top = unrolled(step, tuple(recv_z[0, c, v] for v in range(V)))
        for v in range(V):
            send_z[0, c, v] = top[v]

        @pl.when(iz < nz - 1)
        def _():
            copy_z(0, c).start()

        pack_faces(1, yh, xh)
        start_faces(1, yh, xh)

    def sweep_down(c):
        ys, xs = cut(*CHUNKS[c])

        @pl.when(iz < nz - 1)
        def _():
            copy_z(1, c).wait_recv()

        def step(z, above):
            upper = matvec(lambda a, b: jv[z, 5, a, b, ys, xs], above)
            change = [rv[z, a, ys, xs] + upper[a] for a in range(V)]
            change = matvec(lambda a, b: dv[z, a, b, ys, xs], change)
            result = [sv[z, a, ys, xs] - change[a] for a in range(V)]
            for a in range(V):
                out_ref[z, a, ys, xs] = result[a]
            return tuple(result)

        bottom = unrolled(step, tuple(recv_z[1, c, v] for v in range(V)), upward=False)
        for v in range(V):
            send_z[1, c, v] = bottom[v]

        @pl.when(iz > 0)
        def _():
            copy_z(1, c).start()

    @pl.loop(0, planes)
    def _(z):
        for copy in load_first(z):
            copy.wait()
        interior(z, True)

    @pl.loop(0, planes)
    def _(z):
        for copy in load_lower(z):
            copy.wait()

    for c, (yh, xh) in enumerate(CHUNKS):
        add_halo(0, yh, xh)
        sweep_up(c)

    @pl.loop(0, planes)
    def _(z):
        interior(z, False)

    @pl.loop(0, planes)
    def _(z):
        for copy in load_upper(z):
            copy.wait()

    for c, (yh, xh) in enumerate(CHUNKS):
        add_halo(1, yh, xh)
        sweep_down(c)

    for e in range(2):
        for yh, xh in CHUNKS:

            @pl.when(has_y[yh])
            def _():
                copy_y(e, yh, xh).wait_send()

            @pl.when(has_x[xh])
            def _():
                copy_x(e, yh, xh).wait_send()

    for c in range(len(CHUNKS)):

        @pl.when(iz < nz - 1)
        def _():
            copy_z(0, c).wait_send()

        @pl.when(iz > 0)
        def _():
            copy_z(1, c).wait_send()


def body(sizes, right_side, previous, diag_inverse, jacobians):
    rhs = jnp.transpose(right_side, (0, 2, 1, 3))
    prev = jnp.transpose(previous, (0, 2, 1, 3))
    dinv = jnp.transpose(diag_inverse, (0, 2, 3, 1, 4))
    jac = jnp.transpose(jacobians, (0, 2, 3, 4, 1, 5))
    planes, _, rows, cols = rhs.shape
    faces = planes * V
    n = len(CHUNKS)
    hbm = pl.BlockSpec(memory_space=pltpu.HBM)
    dma = pltpu.SemaphoreType.DMA
    out = pl.pallas_call(
        functools.partial(kernel, sizes),
        out_shape=jax.ShapeDtypeStruct(rhs.shape, F32),
        in_specs=[hbm] * 4,
        out_specs=pl.BlockSpec(memory_space=pltpu.VMEM),
        scratch_shapes=[
            pltpu.VMEM(jac.shape, jac.dtype),
            pltpu.VMEM(dinv.shape, dinv.dtype),
            pltpu.VMEM(rhs.shape, F32),
            pltpu.VMEM(rhs.shape, F32),
            pltpu.VMEM(rhs.shape, F32),
            pltpu.VMEM((2, 2, 2, faces, 1, TILE_X), F32),
            pltpu.VMEM((2, 2, 2, faces, 1, TILE_X), F32),
            pltpu.VMEM((2, 2, 2, TILE_Y, TILE_X), F32),
            pltpu.VMEM((2, 2, 2, TILE_Y, TILE_X), F32),
            pltpu.VMEM((2, n, V, TILE_Y, TILE_X), F32),
            pltpu.VMEM((2, n, V, TILE_Y, TILE_X), F32),
            dma, dma((planes,)), dma((planes,)), dma((planes,)), dma((planes,)), dma((planes,)),
            dma((2, 2, 2)), dma((2, 2, 2)), dma((2, 2, 2)), dma((2, 2, 2)),
            dma((2, n)), dma((2, n)),
        ],
        compiler_params=pltpu.CompilerParams(
            collective_id=0, has_side_effects=True, vmem_limit_bytes=30 * 1024 * 1024),
        name="sweep_pair",
    )(*(pltpu.with_memory_space_constraint(x, pltpu.HBM) for x in (rhs, prev, dinv, jac)))
    return jnp.transpose(out, (0, 2, 1, 3))


def solution(mesh):
    placed = (
        P("gz", "gy", None, "gx"),
        P("gz", "gy", None, "gx"),
        P("gz", "gy", None, None, "gx"),
        P("gz", "gy", None, None, None, "gx"),
    )
    sizes = tuple(mesh.shape[a] for a in ("gz", "gx", "gy"))
    return jax.shard_map(
        functools.partial(body, sizes), mesh=mesh, in_specs=placed,
        out_specs=P("gz", "gy", None, "gx"), check_vma=False,
    )
```

```python
import functools

import jax
import jax.numpy as jnp
from jax import lax
from jax.experimental import pallas as pl
from jax.experimental.pallas import tpu as pltpu
from jax.sharding import PartitionSpec as P

F32 = jnp.float32
V = 6
TILE_Y, TILE_X = 8, 128
PLANES_AT_ONCE = 5
CHUNKS = ((0, 0), (1, 0), (0, 1), (1, 1))


def kernel(sizes, rhs_h, prev_h, dinv_h, jac_h, out_ref, jv, dv, mv, rv, pv, sv,
           send_y, recv_y, send_x, recv_x, send_z, recv_z,
           ld_p, ld_r, ld_j, ld_l, ld_u, ssy, rsy, ssx, rsx, ssz, rsz):
    nz, nx, ny = sizes
    planes, _, rows, cols = rhs_h.shape
    iz, ix, iy = (lax.axis_index(a) for a in ("gz", "gx", "gy"))

    load_prev = pltpu.make_async_copy(prev_h, pv, ld_p)
    load_prev.start()

    def load_first(z):
        return pltpu.make_async_copy(
            jac_h.at[z, pl.ds(0, 4)], jv.at[z, pl.ds(0, 4)], ld_j.at[z])

    @pl.loop(0, planes)
    def _(z):
        load_first(z).start()


    load_rhs = pltpu.make_async_copy(rhs_h, sv, ld_r)

    def load_lower(xh):
        xs = pl.ds(xh * TILE_X, TILE_X)
        return (
            pltpu.make_async_copy(
                jac_h.at[:, 4, :, :, :, xs], jv.at[:, 4, :, :, :, xs], ld_l.at[xh, 0]),
            pltpu.make_async_copy(
                dinv_h.at[:, :, :, :, xs], dv.at[:, :, :, :, xs], ld_l.at[xh, 1]),
        )

    load_upper = pltpu.make_async_copy(jac_h.at[:, 5], jv.at[:, 5], ld_u)
    sides = (
        ("gy", -1, iy > 0), ("gy", 1, iy < ny - 1),
        ("gx", -1, ix > 0), ("gx", 1, ix < nx - 1),
        ("gz", -1, iz > 0), ("gz", 1, iz < nz - 1),
    )
    at = {"gz": iz, "gx": ix, "gy": iy}
    barrier = pltpu.get_barrier_semaphore()
    for axis, step, exists in sides:

        @pl.when(exists)
        def _():
            pl.semaphore_signal(
                barrier, inc=1, device_id={axis: at[axis] + step},
                device_id_type=pl.DeviceIdType.MESH)

    def copy_y(e, yh, xh):
        step = 2 * yh - 1
        return pltpu.make_async_remote_copy(
            send_y.at[e, yh, xh], recv_y.at[e, 1 - yh, xh], ssy.at[e, yh, xh],
            rsy.at[e, 1 - yh, xh], device_id={"gy": iy + step},
            device_id_type=pl.DeviceIdType.MESH)

    def copy_x(e, yh, xh):
        step = 2 * xh - 1
        return pltpu.make_async_remote_copy(
            send_x.at[e, xh, yh], recv_x.at[e, 1 - xh, yh], ssx.at[e, xh, yh],
            rsx.at[e, 1 - xh, yh], device_id={"gx": ix + step},
            device_id_type=pl.DeviceIdType.MESH)

    def copy_z(d, c):
        step = 1 - 2 * d
        return pltpu.make_async_remote_copy(
            send_z.at[d, c], recv_z.at[d, c], ssz.at[d, c], rsz.at[d, c],
            device_id={"gz": iz + step}, device_id_type=pl.DeviceIdType.MESH)

    has_y = (iy > 0, iy < ny - 1)
    has_x = (ix > 0, ix < nx - 1)

    def start_faces(e, yh, xh):
        @pl.when(has_y[yh])
        def _():
            copy_y(e, yh, xh).start()

        @pl.when(has_x[xh])
        def _():
            copy_x(e, yh, xh).start()

    def wait_faces(e, yh, xh):
        @pl.when(has_y[yh])
        def _():
            copy_y(e, 1 - yh, xh).wait_recv()

        @pl.when(has_x[xh])
        def _():
            copy_x(e, yh, 1 - xh).wait_recv()

    lane8 = lax.broadcasted_iota(jnp.int32, (TILE_Y, TILE_X), 1)
    row8 = lax.broadcasted_iota(jnp.int32, (TILE_Y, TILE_X), 0)

    def cut(yh, xh):
        return pl.ds(yh * TILE_Y, TILE_Y), pl.ds(xh * TILE_X, TILE_X)

    def pack_faces(e, yh, xh):
        ys, xs = cut(yh, xh)
        edge = yh * (rows - 1)
        packed = [jnp.zeros((TILE_Y, TILE_X), F32) for _ in range(4)]
        for index in range(planes * V):
            z, v = divmod(index, V)
            send_y[e, yh, xh, index] = pv[z, v, edge:edge + 1, xs]
            turned = pltpu.roll(pv[z, v, ys, xs], index + 2 * xh, 1)
            packed[index % 4] = jnp.where(lane8 == index + xh, turned, packed[index % 4])
        send_x[e, xh, yh] = (packed[0] + packed[1]) + (packed[2] + packed[3])

    def unrolled(step, carry, upward=True):
        def turn(i, carry):
            for j in range(PLANES_AT_ONCE):
                at = i * PLANES_AT_ONCE + j
                carry = step(at if upward else planes - 1 - at, carry)
            return carry

        return lax.fori_loop(0, planes // PLANES_AT_ONCE, turn, carry)

    load_prev.wait()
    for copy in (load_rhs,) + load_lower(0):
        copy.start()

    for yh, xh in CHUNKS:
        pack_faces(0, yh, xh)

    pl.semaphore_wait(barrier, sum(exists.astype(jnp.int32) for _, _, exists in sides))

    for yh, xh in CHUNKS:
        start_faces(0, yh, xh)

    for side in range(2):

        @pl.when(jnp.logical_not(has_y[side]))
        def _():
            for e in range(2):
                for xh in range(2):
                    recv_y[e, side, xh] = jnp.zeros(recv_y.shape[3:], F32)

        @pl.when(jnp.logical_not(has_x[side]))
        def _():
            for e in range(2):
                for yh in range(2):
                    recv_x[e, side, yh] = jnp.zeros(recv_x.shape[3:], F32)

    @pl.when(iz == 0)
    def _():
        recv_z[0] = jnp.zeros(recv_z.shape[1:], F32)

    @pl.when(iz == nz - 1)
    def _():
        recv_z[1] = jnp.zeros(recv_z.shape[1:], F32)

    lane = lax.broadcasted_iota(jnp.int32, (rows, cols), 1)
    row = lax.broadcasted_iota(jnp.int32, (rows, cols), 0)
    shifts = (
        (lane == 0, 1, 1), (lane == cols - 1, cols - 1, 1),
        (row == 0, 1, 0), (row == rows - 1, rows - 1, 0),
    )

    def interior(z):
        f = [pv[z, v] for v in range(V)]
        for n, (edge, shift, axis) in enumerate(shifts):
            g = [jnp.where(edge, 0.0, pltpu.roll(x, shift, axis)) for x in f]
            for a in range(V):
                total = jv[z, n, a, 0].astype(F32) * g[0]
                for b in range(1, V):
                    total = total + jv[z, n, a, b].astype(F32) * g[b]
                if n == 0:
                    rv[z, a] = total
                else:
                    rv[z, a] = rv[z, a] + total

    def matvec(blocks, vector):
        out = []
        for a in range(V):
            terms = [blocks(a, b).astype(F32) * vector[b] for b in range(V)]
            out.append(((terms[0] + terms[1]) + (terms[2] + terms[3])) + (terms[4] + terms[5]))
        return out

    def add_halo(e, yh, xh):
        ys, xs = cut(yh, xh)
        wait_faces(e, yh, xh)
        packed = recv_x[e, xh, yh]
        on_row = row8 == (TILE_Y - 1) * yh
        on_lane = lane8 == (TILE_X - 1) * xh

        def step(z, carry):
            hy, hx = [], []
            for v in range(V):
                index = z * V + v
                hy.append(jnp.where(on_row, recv_y[e, yh, xh, index], 0.0))
                hx.append(jnp.where(on_lane, pltpu.roll(packed, TILE_X - 1 - index, 1), 0.0))
            fx = matvec(lambda a, b: jv[z, xh, a, b, ys, xs], hx)
            fy = matvec(lambda a, b: jv[z, 2 + yh, a, b, ys, xs], hy)
            for a in range(V):
                if e == 0:
                    rv[z, a, ys, xs] = sv[z, a, ys, xs] - (rv[z, a, ys, xs] + (fx[a] + fy[a]))
                else:
                    rv[z, a, ys, xs] = rv[z, a, ys, xs] + (fx[a] + fy[a])
            return carry

        unrolled(step, 0)

    def sweep_up(c):
        yh, xh = CHUNKS[c]
        ys, xs = cut(yh, xh)

        @pl.when(iz > 0)
        def _():
            copy_z(0, c).wait_recv()

        def step(z, below):
            lower = matvec(lambda a, b: jv[z, 4, a, b, ys, xs], below)
            source = [rv[z, a, ys, xs] - lower[a] for a in range(V)]
            result = matvec(lambda a, b: dv[z, a, b, ys, xs], source)
            for a in range(V):
                sv[z, a, ys, xs] = result[a]
                pv[z, a, ys, xs] = result[a] - pv[z, a, ys, xs]
            return tuple(result)

        top = unrolled(step, tuple(recv_z[0, c, v] for v in range(V)))
        for v in range(V):
            send_z[0, c, v] = top[v]

        @pl.when(iz < nz - 1)
        def _():
            copy_z(0, c).start()

        @pl.when(iz == nz - 1)
        def _():
            pack_faces(1, yh, xh)
            start_faces(1, yh, xh)

    def finish_down(c, step):
        bottom = unrolled(step, tuple(recv_z[1, c, v] for v in range(V)), upward=False)
        for v in range(V):
            send_z[1, c, v] = bottom[v]

        @pl.when(iz > 0)
        def _():
            copy_z(1, c).start()

    def sweep_down(c):
        ys, xs = cut(*CHUNKS[c])

        def step(z, above):
            upper = matvec(lambda a, b: jv[z, 5, a, b, ys, xs], above)
            change = [rv[z, a, ys, xs] + upper[a] for a in range(V)]
            change = matvec(lambda a, b: dv[z, a, b, ys, xs], change)
            result = [sv[z, a, ys, xs] - change[a] for a in range(V)]
            for a in range(V):
                out_ref[z, a, ys, xs] = result[a]
            return tuple(result)

        finish_down(c, step)

    def fold(c):
        ys, xs = cut(*CHUNKS[c])

        @pl.loop(0, planes)
        def _(z):
            inner = [rv[z, b, ys, xs] for b in range(V)]
            upper = [[jv[z, 5, k, b, ys, xs].astype(F32) for b in range(V)] for k in range(V)]
            for a in range(V):
                inverse = [dv[z, a, k, ys, xs].astype(F32) for k in range(V)]
                for b in range(V):
                    terms = [inverse[k] * upper[k][b] for k in range(V)]
                    mv[z, a, b, ys, xs] = (
                        ((terms[0] + terms[1]) + (terms[2] + terms[3])) + (terms[4] + terms[5]))
                terms = [inverse[k] * inner[k] for k in range(V)]
                sv[z, a, ys, xs] = sv[z, a, ys, xs] - (
                    ((terms[0] + terms[1]) + (terms[2] + terms[3])) + (terms[4] + terms[5]))

    def sweep_down_folded(c):
        ys, xs = cut(*CHUNKS[c])
        copy_z(1, c).wait_recv()

        def step(z, above):
            change = matvec(lambda a, b: mv[z, a, b, ys, xs], above)
            result = [sv[z, a, ys, xs] - change[a] for a in range(V)]
            for a in range(V):
                out_ref[z, a, ys, xs] = result[a]
            return tuple(result)

        finish_down(c, step)

    @pl.loop(0, planes)
    def _(z):
        load_first(z).wait()
        interior(z)

    for copy in load_lower(1) + (load_upper,):
        copy.start()

    for c, (yh, xh) in enumerate(CHUNKS):
        if c == 0:
            load_rhs.wait()
        if yh == 0:
            for copy in load_lower(xh):
                copy.wait()
        add_halo(0, yh, xh)
        sweep_up(c)

    @pl.when(iz < nz - 1)
    def _():
        for yh, xh in CHUNKS:
            pack_faces(1, yh, xh)
            start_faces(1, yh, xh)

    @pl.loop(0, planes)
    def _(z):
        interior(z)

    load_upper.wait()

    @pl.when(iz == nz - 1)
    def _():
        for c, (yh, xh) in enumerate(CHUNKS):
            add_halo(1, yh, xh)
            sweep_down(c)

    @pl.when(iz < nz - 1)
    def _():
        for c, (yh, xh) in enumerate(CHUNKS):
            add_halo(1, yh, xh)
            fold(c)
        for c in range(len(CHUNKS)):
            sweep_down_folded(c)

    for e in range(2):
        for yh, xh in CHUNKS:

            @pl.when(has_y[yh])
            def _():
                copy_y(e, yh, xh).wait_send()

            @pl.when(has_x[xh])
            def _():
                copy_x(e, yh, xh).wait_send()

    for c in range(len(CHUNKS)):

        @pl.when(iz < nz - 1)
        def _():
            copy_z(0, c).wait_send()

        @pl.when(iz > 0)
        def _():
            copy_z(1, c).wait_send()


def body(sizes, right_side, previous, diag_inverse, jacobians):
    rhs = jnp.transpose(right_side, (0, 2, 1, 3))
    prev = jnp.transpose(previous, (0, 2, 1, 3))
    dinv = jnp.transpose(diag_inverse, (0, 2, 3, 1, 4))
    jac = jnp.transpose(jacobians, (0, 2, 3, 4, 1, 5))
    planes, _, rows, cols = rhs.shape
    faces = planes * V
    n = len(CHUNKS)
    hbm = pl.BlockSpec(memory_space=pltpu.HBM)
    dma = pltpu.SemaphoreType.DMA
    out = pl.pallas_call(
        functools.partial(kernel, sizes),
        out_shape=jax.ShapeDtypeStruct(rhs.shape, F32),
        in_specs=[hbm] * 4,
        out_specs=pl.BlockSpec(memory_space=pltpu.VMEM),
        scratch_shapes=[
            pltpu.VMEM(jac.shape, jac.dtype),
            pltpu.VMEM(dinv.shape, dinv.dtype),
            pltpu.VMEM(dinv.shape, F32),
            pltpu.VMEM(rhs.shape, F32),
            pltpu.VMEM(rhs.shape, F32),
            pltpu.VMEM(rhs.shape, F32),
            pltpu.VMEM((2, 2, 2, faces, 1, TILE_X), F32),
            pltpu.VMEM((2, 2, 2, faces, 1, TILE_X), F32),
            pltpu.VMEM((2, 2, 2, TILE_Y, TILE_X), F32),
            pltpu.VMEM((2, 2, 2, TILE_Y, TILE_X), F32),
            pltpu.VMEM((2, n, V, TILE_Y, TILE_X), F32),
            pltpu.VMEM((2, n, V, TILE_Y, TILE_X), F32),
            dma, dma, dma((planes,)), dma((2, 2)), dma,
            dma((2, 2, 2)), dma((2, 2, 2)), dma((2, 2, 2)), dma((2, 2, 2)),
            dma((2, n)), dma((2, n)),
        ],
        compiler_params=pltpu.CompilerParams(
            collective_id=0, has_side_effects=True, vmem_limit_bytes=40 * 1024 * 1024),
        name="sweep_pair",
    )(*(pltpu.with_memory_space_constraint(x, pltpu.HBM) for x in (rhs, prev, dinv, jac)))
    return jnp.transpose(out, (0, 2, 1, 3))


def solution(mesh):
    placed = (
        P("gz", "gy", None, "gx"),
        P("gz", "gy", None, "gx"),
        P("gz", "gy", None, None, "gx"),
        P("gz", "gy", None, None, None, "gx"),
    )
    sizes = tuple(mesh.shape[a] for a in ("gz", "gx", "gy"))
    return jax.shard_map(
        functools.partial(body, sizes), mesh=mesh, in_specs=placed,
        out_specs=P("gz", "gy", None, "gx"), check_vma=False,
    )
```

```python
import functools

import jax
import jax.numpy as jnp
from jax import lax
from jax.experimental import pallas as pl
from jax.experimental.pallas import tpu as pltpu
from jax.sharding import PartitionSpec as P

F32 = jnp.float32
V = 6
TILE_Y, TILE_X = 8, 128
PLANES_AT_ONCE = 10
CHUNKS = ((0, 0), (1, 0), (0, 1), (1, 1))


def kernel(sizes, rhs_h, prev_h, dinv_h, jac_h, out_ref, jv, dv, mv, rv, pv, sv,
           send_y, recv_y, send_x, recv_x, send_z, recv_z,
           ld_p, ld_r, ld_j, ld_l, ld_u, ssy, rsy, ssx, rsx, ssz, rsz):
    nz, nx, ny = sizes
    planes, _, rows, cols = rhs_h.shape
    iz, ix, iy = (lax.axis_index(a) for a in ("gz", "gx", "gy"))

    load_prev = pltpu.make_async_copy(prev_h, pv, ld_p)
    load_prev.start()

    def load_first(z):
        return pltpu.make_async_copy(
            jac_h.at[z, pl.ds(0, 4)], jv.at[z, pl.ds(0, 4)], ld_j.at[z])

    @pl.loop(0, planes)
    def _(z):
        load_first(z).start()


    load_rhs = pltpu.make_async_copy(rhs_h, sv, ld_r)

    def load_lower(xh):
        xs = pl.ds(xh * TILE_X, TILE_X)
        return (
            pltpu.make_async_copy(
                jac_h.at[:, 4, :, :, :, xs], jv.at[:, 4, :, :, :, xs], ld_l.at[xh, 0]),
            pltpu.make_async_copy(
                dinv_h.at[:, :, :, :, xs], dv.at[:, :, :, :, xs], ld_l.at[xh, 1]),
        )

    load_upper = pltpu.make_async_copy(jac_h.at[:, 5], jv.at[:, 5], ld_u)
    sides = (
        ("gy", -1, iy > 0), ("gy", 1, iy < ny - 1),
        ("gx", -1, ix > 0), ("gx", 1, ix < nx - 1),
        ("gz", -1, iz > 0), ("gz", 1, iz < nz - 1),
    )
    at = {"gz": iz, "gx": ix, "gy": iy}
    barrier = pltpu.get_barrier_semaphore()
    for axis, step, exists in sides:

        @pl.when(exists)
        def _():
            pl.semaphore_signal(
                barrier, inc=1, device_id={axis: at[axis] + step},
                device_id_type=pl.DeviceIdType.MESH)

    def copy_y(e, yh, xh):
        step = 2 * yh - 1
        return pltpu.make_async_remote_copy(
            send_y.at[e, yh, xh], recv_y.at[e, 1 - yh, xh], ssy.at[e, yh, xh],
            rsy.at[e, 1 - yh, xh], device_id={"gy": iy + step},
            device_id_type=pl.DeviceIdType.MESH)

    def copy_x(e, yh, xh):
        step = 2 * xh - 1
        return pltpu.make_async_remote_copy(
            send_x.at[e, xh, yh], recv_x.at[e, 1 - xh, yh], ssx.at[e, xh, yh],
            rsx.at[e, 1 - xh, yh], device_id={"gx": ix + step},
            device_id_type=pl.DeviceIdType.MESH)

    def copy_z(d, c):
        step = 1 - 2 * d
        return pltpu.make_async_remote_copy(
            send_z.at[d, c], recv_z.at[d, c], ssz.at[d, c], rsz.at[d, c],
            device_id={"gz": iz + step}, device_id_type=pl.DeviceIdType.MESH)

    has_y = (iy > 0, iy < ny - 1)
    has_x = (ix > 0, ix < nx - 1)

    def start_faces(e, yh, xh):
        @pl.when(has_x[xh])
        def _():
            copy_x(e, yh, xh).start()

        @pl.when(has_y[yh])
        def _():
            copy_y(e, yh, xh).start()

    def wait_faces(e, yh, xh):
        @pl.when(has_y[yh])
        def _():
            copy_y(e, 1 - yh, xh).wait_recv()

        @pl.when(has_x[xh])
        def _():
            copy_x(e, yh, 1 - xh).wait_recv()

    lane8 = lax.broadcasted_iota(jnp.int32, (TILE_Y, TILE_X), 1)
    row8 = lax.broadcasted_iota(jnp.int32, (TILE_Y, TILE_X), 0)

    def cut(yh, xh):
        return pl.ds(yh * TILE_Y, TILE_Y), pl.ds(xh * TILE_X, TILE_X)

    def pack_faces(e, yh, xh):
        ys, xs = cut(yh, xh)
        edge = yh * (rows - 1)
        packed = [jnp.zeros((TILE_Y, TILE_X), F32) for _ in range(4)]
        for index in range(planes * V):
            z, v = divmod(index, V)
            send_y[e, yh, xh, index] = pv[z, v, edge:edge + 1, xs]
            turned = pltpu.roll(pv[z, v, ys, xs], index + 2 * xh, 1)
            packed[index % 4] = jnp.where(lane8 == index + xh, turned, packed[index % 4])
        send_x[e, xh, yh] = (packed[0] + packed[1]) + (packed[2] + packed[3])

    def unrolled(step, carry, upward=True):
        def turn(i, carry):
            for j in range(PLANES_AT_ONCE):
                at = i * PLANES_AT_ONCE + j
                carry = step(at if upward else planes - 1 - at, carry)
            return carry

        return lax.fori_loop(0, planes // PLANES_AT_ONCE, turn, carry)

    load_prev.wait()
    for copy in (load_rhs,) + load_lower(0):
        copy.start()

    for yh, xh in CHUNKS:
        pack_faces(0, yh, xh)

    pl.semaphore_wait(barrier, sum(exists.astype(jnp.int32) for _, _, exists in sides))

    for yh, xh in CHUNKS:
        start_faces(0, yh, xh)

    for side in range(2):

        @pl.when(jnp.logical_not(has_y[side]))
        def _():
            for e in range(2):
                for xh in range(2):
                    recv_y[e, side, xh] = jnp.zeros(recv_y.shape[3:], F32)

        @pl.when(jnp.logical_not(has_x[side]))
        def _():
            for e in range(2):
                for yh in range(2):
                    recv_x[e, side, yh] = jnp.zeros(recv_x.shape[3:], F32)

    @pl.when(iz == 0)
    def _():
        recv_z[0] = jnp.zeros(recv_z.shape[1:], F32)

    @pl.when(iz == nz - 1)
    def _():
        recv_z[1] = jnp.zeros(recv_z.shape[1:], F32)

    lane = lax.broadcasted_iota(jnp.int32, (rows, cols), 1)
    row = lax.broadcasted_iota(jnp.int32, (rows, cols), 0)
    shifts = (
        (lane == 0, 1, 1), (lane == cols - 1, cols - 1, 1),
        (row == 0, 1, 0), (row == rows - 1, rows - 1, 0),
    )

    def interior(z):
        f = [pv[z, v] for v in range(V)]
        for n, (edge, shift, axis) in enumerate(shifts):
            g = [jnp.where(edge, 0.0, pltpu.roll(x, shift, axis)) for x in f]
            for a in range(V):
                total = jv[z, n, a, 0].astype(F32) * g[0]
                for b in range(1, V):
                    total = total + jv[z, n, a, b].astype(F32) * g[b]
                if n == 0:
                    rv[z, a] = total
                else:
                    rv[z, a] = rv[z, a] + total

    def matvec(blocks, vector):
        out = []
        for a in range(V):
            terms = [blocks(a, b).astype(F32) * vector[b] for b in range(V)]
            out.append(((terms[0] + terms[1]) + (terms[2] + terms[3])) + (terms[4] + terms[5]))
        return out

    def add_halo(e, yh, xh):
        ys, xs = cut(yh, xh)
        wait_faces(e, yh, xh)
        packed = recv_x[e, xh, yh]
        on_row = row8 == (TILE_Y - 1) * yh
        on_lane = lane8 == (TILE_X - 1) * xh

        def step(z, carry):
            hy, hx = [], []
            for v in range(V):
                index = z * V + v
                hy.append(jnp.where(on_row, recv_y[e, yh, xh, index], 0.0))
                hx.append(jnp.where(on_lane, pltpu.roll(packed, TILE_X - 1 - index, 1), 0.0))
            fx = matvec(lambda a, b: jv[z, xh, a, b, ys, xs], hx)
            fy = matvec(lambda a, b: jv[z, 2 + yh, a, b, ys, xs], hy)
            for a in range(V):
                if e == 0:
                    rv[z, a, ys, xs] = sv[z, a, ys, xs] - (rv[z, a, ys, xs] + (fx[a] + fy[a]))
                else:
                    rv[z, a, ys, xs] = rv[z, a, ys, xs] + (fx[a] + fy[a])
            return carry

        unrolled(step, 0)

    def sweep_up(c):
        yh, xh = CHUNKS[c]
        ys, xs = cut(yh, xh)

        @pl.when(iz > 0)
        def _():
            copy_z(0, c).wait_recv()

        def step(z, below):
            lower = matvec(lambda a, b: jv[z, 4, a, b, ys, xs], below)
            source = [rv[z, a, ys, xs] - lower[a] for a in range(V)]
            result = matvec(lambda a, b: dv[z, a, b, ys, xs], source)
            for a in range(V):
                sv[z, a, ys, xs] = result[a]
                pv[z, a, ys, xs] = result[a] - pv[z, a, ys, xs]
            return tuple(result)

        top = unrolled(step, tuple(recv_z[0, c, v] for v in range(V)))
        for v in range(V):
            send_z[0, c, v] = top[v]

        @pl.when(iz < nz - 1)
        def _():
            copy_z(0, c).start()

        @pl.when(iz == nz - 1)
        def _():
            pack_faces(1, yh, xh)
            start_faces(1, yh, xh)

    def finish_down(c, step):
        bottom = unrolled(step, tuple(recv_z[1, c, v] for v in range(V)), upward=False)
        for v in range(V):
            send_z[1, c, v] = bottom[v]

        @pl.when(iz > 0)
        def _():
            copy_z(1, c).start()

    def sweep_down(c):
        ys, xs = cut(*CHUNKS[c])

        def step(z, above):
            upper = matvec(lambda a, b: jv[z, 5, a, b, ys, xs], above)
            change = [rv[z, a, ys, xs] + upper[a] for a in range(V)]
            change = matvec(lambda a, b: dv[z, a, b, ys, xs], change)
            result = [sv[z, a, ys, xs] - change[a] for a in range(V)]
            for a in range(V):
                out_ref[z, a, ys, xs] = result[a]
            return tuple(result)

        finish_down(c, step)

    def fold(c):
        ys, xs = cut(*CHUNKS[c])

        @pl.loop(0, planes)
        def _(z):
            inner = [rv[z, b, ys, xs] for b in range(V)]
            upper = [[jv[z, 5, k, b, ys, xs].astype(F32) for b in range(V)] for k in range(V)]
            for a in range(V):
                inverse = [dv[z, a, k, ys, xs].astype(F32) for k in range(V)]
                for b in range(V):
                    terms = [inverse[k] * upper[k][b] for k in range(V)]
                    mv[z, a, b, ys, xs] = (
                        ((terms[0] + terms[1]) + (terms[2] + terms[3])) + (terms[4] + terms[5]))
                terms = [inverse[k] * inner[k] for k in range(V)]
                sv[z, a, ys, xs] = sv[z, a, ys, xs] - (
                    ((terms[0] + terms[1]) + (terms[2] + terms[3])) + (terms[4] + terms[5]))

    def sweep_down_folded(c):
        ys, xs = cut(*CHUNKS[c])
        copy_z(1, c).wait_recv()

        def step(z, above):
            change = matvec(lambda a, b: mv[z, a, b, ys, xs], above)
            result = [sv[z, a, ys, xs] - change[a] for a in range(V)]
            for a in range(V):
                out_ref[z, a, ys, xs] = result[a]
            return tuple(result)

        finish_down(c, step)

    @pl.loop(0, planes)
    def _(z):
        load_first(z).wait()
        interior(z)

    for copy in load_lower(1) + (load_upper,):
        copy.start()

    for c, (yh, xh) in enumerate(CHUNKS):
        if c == 0:
            load_rhs.wait()
        if yh == 0:
            for copy in load_lower(xh):
                copy.wait()
        add_halo(0, yh, xh)
        sweep_up(c)

    @pl.when(iz < nz - 1)
    def _():
        for yh, xh in CHUNKS:
            pack_faces(1, yh, xh)
            start_faces(1, yh, xh)

    @pl.loop(0, planes)
    def _(z):
        interior(z)

    load_upper.wait()

    @pl.when(iz == nz - 1)
    def _():
        for c, (yh, xh) in enumerate(CHUNKS):
            add_halo(1, yh, xh)
            sweep_down(c)

    @pl.when(iz < nz - 1)
    def _():
        for c, (yh, xh) in enumerate(CHUNKS):
            add_halo(1, yh, xh)
            fold(c)
        for c in range(len(CHUNKS)):
            sweep_down_folded(c)

    for e in range(2):
        for yh, xh in CHUNKS:

            @pl.when(has_y[yh])
            def _():
                copy_y(e, yh, xh).wait_send()

            @pl.when(has_x[xh])
            def _():
                copy_x(e, yh, xh).wait_send()

    for c in range(len(CHUNKS)):

        @pl.when(iz < nz - 1)
        def _():
            copy_z(0, c).wait_send()

        @pl.when(iz > 0)
        def _():
            copy_z(1, c).wait_send()


def body(sizes, right_side, previous, diag_inverse, jacobians):
    rhs = jnp.transpose(right_side, (0, 2, 1, 3))
    prev = jnp.transpose(previous, (0, 2, 1, 3))
    dinv = jnp.transpose(diag_inverse, (0, 2, 3, 1, 4))
    jac = jnp.transpose(jacobians, (0, 2, 3, 4, 1, 5))
    planes, _, rows, cols = rhs.shape
    faces = planes * V
    n = len(CHUNKS)
    hbm = pl.BlockSpec(memory_space=pltpu.HBM)
    dma = pltpu.SemaphoreType.DMA
    out = pl.pallas_call(
        functools.partial(kernel, sizes),
        out_shape=jax.ShapeDtypeStruct(rhs.shape, F32),
        in_specs=[hbm] * 4,
        out_specs=pl.BlockSpec(memory_space=pltpu.VMEM),
        scratch_shapes=[
            pltpu.VMEM(jac.shape, jac.dtype),
            pltpu.VMEM(dinv.shape, dinv.dtype),
            pltpu.VMEM(dinv.shape, F32),
            pltpu.VMEM(rhs.shape, F32),
            pltpu.VMEM(rhs.shape, F32),
            pltpu.VMEM(rhs.shape, F32),
            pltpu.VMEM((2, 2, 2, faces, 1, TILE_X), F32),
            pltpu.VMEM((2, 2, 2, faces, 1, TILE_X), F32),
            pltpu.VMEM((2, 2, 2, TILE_Y, TILE_X), F32),
            pltpu.VMEM((2, 2, 2, TILE_Y, TILE_X), F32),
            pltpu.VMEM((2, n, V, TILE_Y, TILE_X), F32),
            pltpu.VMEM((2, n, V, TILE_Y, TILE_X), F32),
            dma, dma, dma((planes,)), dma((2, 2)), dma,
            dma((2, 2, 2)), dma((2, 2, 2)), dma((2, 2, 2)), dma((2, 2, 2)),
            dma((2, n)), dma((2, n)),
        ],
        compiler_params=pltpu.CompilerParams(
            collective_id=0, has_side_effects=True, vmem_limit_bytes=40 * 1024 * 1024),
        name="sweep_pair",
    )(*(pltpu.with_memory_space_constraint(x, pltpu.HBM) for x in (rhs, prev, dinv, jac)))
    return jnp.transpose(out, (0, 2, 1, 3))


def solution(mesh):
    placed = (
        P("gz", "gy", None, "gx"),
        P("gz", "gy", None, "gx"),
        P("gz", "gy", None, None, "gx"),
        P("gz", "gy", None, None, None, "gx"),
    )
    sizes = tuple(mesh.shape[a] for a in ("gz", "gx", "gy"))
    return jax.shard_map(
        functools.partial(body, sizes), mesh=mesh, in_specs=placed,
        out_specs=P("gz", "gy", None, "gx"), check_vma=False,
    )
```
